512 devices in a mesh: head: 2 (over core), seq: 256 (over z, y, x).
Axes of the slice: x: 4, y: 8, z: 8, core: 2. Of those that a mesh axis runs over, the one named last changes fastest.
Arguments:
- query_matrix: bfloat16 [32, 32768, 128], P(None, ('seq', 'head')), may hold values from -6 to 6
- key_matrix: bfloat16 [8, 32768, 128], P(None, ('seq', 'head')), may hold values from -6 to 6
- value_matrix: bfloat16 [8, 32768, 128], P(None, ('seq', 'head')), may hold values from -6 to 6
- output_gradient: bfloat16 [32, 32768, 128], P(None, ('seq', 'head')), may hold values from -6 to 6
- query_head_spans: int32 [32], replicated, may hold values from 64 to 256, as said below
- slab_offset: int32 [1], replicated, may hold values from 0 to 8191
Outputs:
- attn_out: bfloat16 [32, 32768, 128], P(None, ('seq', 'head'))
- query_grad: bfloat16 [32, 32768, 128], P(None, ('seq', 'head'))
- key_grad: bfloat16 [8, 32768, 128], P(None, ('seq', 'head'))
- value_grad: bfloat16 [8, 32768, 128], P(None, ('seq', 'head'))
The draws below stay inside these ranges and needn't reach their ends.
Inputs may be any that keep to these rules, and one draw needn't show every extreme that they name: `query_head_spans`: every span is a multiple of 64; some head has the span 4 * 64 and some head the span 64.
All inputs are finite; a program needn't handle non-finite values.
Results may differ from the reference program's by a relative error of at most 0.019.
Values may be sent and summed in bfloat16 or wider, within the bound.
A program may use at most 64 MiB of HBM per device.

```python
import jax
import jax.numpy as jnp
from jax import lax

QUERY_HEADS = 32
KEY_VALUE_HEADS = 8
HEAD_WIDTH = 128
TOK_SEQ = 128
LEVELS = 4
SPAN_UNIT = 64
REACH = 2
SEGMENT = 512
SLAB_TOKENS = 32768
N_SEQ = 256


def shared_rows(key):
    query_shape = (QUERY_HEADS, SLAB_TOKENS, HEAD_WIDTH)
    key_array_shape = (KEY_VALUE_HEADS, SLAB_TOKENS, HEAD_WIDTH)
    query_base = jnp.clip(jax.random.normal(jax.random.fold_in(key, 11), query_shape, jnp.float32), -6.0, 6.0)
    key_start_index = jnp.clip(jax.random.normal(jax.random.fold_in(key, 12), key_array_shape, jnp.float32), -6.0, 6.0)
    return (query_base, key_start_index)


def draw_query_matrix(key, part):
    return shared_rows(key)[0].astype(jnp.bfloat16)


def draw_key_matrix(key, part):
    return shared_rows(key)[1].astype(jnp.bfloat16)


def draw_query_head_spans(key, part):
    levels = jax.random.randint(jax.random.fold_in(key, 21), (QUERY_HEADS,), 1, LEVELS + 1)
    longest = jax.random.randint(jax.random.fold_in(key, 22), (), 0, QUERY_HEADS)
    shortest = (longest + jax.random.randint(jax.random.fold_in(key, 23), (), 1, QUERY_HEADS)) % QUERY_HEADS
    levels = levels.at[longest].set(LEVELS).at[shortest].set(1)
    return (levels * SPAN_UNIT).astype(jnp.int32)


def block_levels(rng, shape, pieces, smallest, high):
    level, own = 1.0, jax.random.fold_in(rng, 6)
    for dim, shards_of in pieces:
        draws = jnp.exp(jax.random.uniform(jax.random.fold_in(own, dim), (shards_of,), jnp.float32, smallest / len(pieces), high / len(pieces)))
        level = level * jnp.repeat(draws, shape[dim] // shards_of).reshape([-1 if axis == dim else 1 for axis in range(len(shape))])
    return level


def bell_draw(key, extent, width, reach, shards=(), kind=jnp.bfloat16):
    result = width * jax.random.normal(key, extent, jnp.float32)
    if shards:
        result = result * block_levels(key, extent, shards, -0.22, 0.18)
    return jnp.clip(result, -reach, reach).astype(kind)


def setup_inputs(seed: int = 0) -> dict:
    key_list = jax.random.split(jax.random.key(seed), 7)
    query_matrix = draw_query_matrix(jax.random.fold_in(key_list[6], 71), 0)
    key_matrix = draw_key_matrix(jax.random.fold_in(key_list[6], 71), 0)
    value_matrix = bell_draw(key_list[2], (KEY_VALUE_HEADS, SLAB_TOKENS, HEAD_WIDTH), 1.0, 6.0, ((1, 512),))
    output_gradient = bell_draw(key_list[3], (QUERY_HEADS, SLAB_TOKENS, HEAD_WIDTH), 1.0, 6.0, ((1, 512),))
    query_head_spans = draw_query_head_spans(jax.random.fold_in(key_list[6], 71), 0)
    slab_offset = jax.random.randint(key_list[5], (1,), 0, 64 * TOK_SEQ).astype(jnp.int32)
    return dict(query_matrix=query_matrix, key_matrix=key_matrix, value_matrix=value_matrix, output_gradient=output_gradient, query_head_spans=query_head_spans, slab_offset=slab_offset)


masked_score = -1e30


def visible_pairs(query_pos, key_pos, span_per_row, doc_offset):
    distance = query_pos[:, None] - key_pos[None, :]
    same_segment = (doc_offset + key_pos[None, :]) // SEGMENT == (doc_offset + query_pos[:, None]) // SEGMENT
    inside = (distance >= 0) & (key_pos[None, :] >= 0) & same_segment
    return inside[None, None] & (distance[None, None] < span_per_row)


def round_half(values):
    return lax.optimization_barrier(values.astype(jnp.bfloat16)).astype(jnp.float32)


def reference(query_matrix, key_matrix, value_matrix, output_gradient, query_head_spans, slab_offset):
    heads_per_group = QUERY_HEADS // KEY_VALUE_HEADS
    score_scale = HEAD_WIDTH ** -0.5
    block_length = TOK_SEQ
    padding_width = REACH * block_length
    key_length = (REACH + 1) * block_length
    doc_offset = slab_offset[0]
    span_per_row = query_head_spans.reshape(KEY_VALUE_HEADS, heads_per_group, 1, 1)
    empty_row_block = jnp.zeros((KEY_VALUE_HEADS, padding_width, HEAD_WIDTH), key_matrix.dtype)
    key_pad = jnp.concatenate([empty_row_block, key_matrix], axis=1)
    value_pad = jnp.concatenate([empty_row_block, value_matrix], axis=1)

    def one_block(carried, block_idx):
        key_acc, value_acc = carried
        start_row = (block_idx * block_length).astype(jnp.int32)
        query_block = lax.dynamic_slice_in_dim(query_matrix, start_row, block_length, 1).reshape(KEY_VALUE_HEADS, heads_per_group, block_length, HEAD_WIDTH).astype(jnp.float32)
        gradient_block = lax.dynamic_slice_in_dim(output_gradient, start_row, block_length, 1).reshape(KEY_VALUE_HEADS, heads_per_group, block_length, HEAD_WIDTH).astype(jnp.float32)
        key_blk = lax.dynamic_slice_in_dim(key_pad, start_row, key_length, 1).astype(jnp.float32)
        value_blk = lax.dynamic_slice_in_dim(value_pad, start_row, key_length, 1).astype(jnp.float32)
        query_pos = start_row + jnp.arange(block_length, dtype=jnp.int32)
        key_pos = start_row - padding_width + jnp.arange(key_length, dtype=jnp.int32)
        visible = visible_pairs(query_pos, key_pos, span_per_row, doc_offset)
        scores = jnp.einsum("gaqd,gkd->gaqk", query_block, key_blk) * score_scale
        row_max = jnp.max(jnp.where(visible, scores, masked_score), axis=-1, keepdims=True)
        weights = jnp.where(visible, jnp.exp(scores - row_max), 0.0)
        row_sum = jnp.sum(weights, axis=-1, keepdims=True)
        weighted = jnp.einsum("gaqk,gkd->gaqd", round_half(weights), value_blk)
        out_blk = (weighted / row_sum).astype(jnp.bfloat16)
        log_total = row_max + jnp.log(row_sum)
        prob_rows = jnp.where(visible, jnp.exp(scores - log_total), 0.0)
        value_part = jnp.einsum("gaqk,gaqd->gkd", round_half(prob_rows), gradient_block)
        prob_grad = jnp.einsum("gaqd,gkd->gaqk", gradient_block, value_blk)
        row_delta = jnp.sum(gradient_block * out_blk.astype(jnp.float32), axis=-1, keepdims=True)
        score_grad = round_half(prob_rows * (prob_grad - row_delta) * score_scale)
        query_part = jnp.einsum("gaqk,gkd->gaqd", score_grad, key_blk).astype(jnp.bfloat16)
        key_part = jnp.einsum("gaqk,gaqd->gkd", score_grad, query_block)
        key_acc = lax.dynamic_update_slice_in_dim(key_acc, lax.dynamic_slice_in_dim(key_acc, start_row, key_length, 1) + key_part, start_row, 1)
        value_acc = lax.dynamic_update_slice_in_dim(value_acc, lax.dynamic_slice_in_dim(value_acc, start_row, key_length, 1) + value_part, start_row, 1)
        return (key_acc, value_acc), (out_blk.reshape(QUERY_HEADS, block_length, HEAD_WIDTH), query_part.reshape(QUERY_HEADS, block_length, HEAD_WIDTH))

    empty_accumulator = jnp.zeros((KEY_VALUE_HEADS, padding_width + SLAB_TOKENS, HEAD_WIDTH), jnp.float32)
    sums, blocks = lax.scan(one_block, (empty_accumulator, empty_accumulator), jnp.arange(N_SEQ, dtype=jnp.int32))
    out_blocks, query_blocks = blocks
    attn_out = jnp.transpose(out_blocks, (1, 0, 2, 3)).reshape(QUERY_HEADS, SLAB_TOKENS, HEAD_WIDTH)
    query_grad = jnp.transpose(query_blocks, (1, 0, 2, 3)).reshape(QUERY_HEADS, SLAB_TOKENS, HEAD_WIDTH)
    key_grad = sums[0][:, padding_width:].astype(jnp.bfloat16)
    value_grad = sums[1][:, padding_width:].astype(jnp.bfloat16)
    return attn_out, query_grad, key_grad, value_grad
```

```python
import jax
import jax.numpy as jnp
from jax import lax
from jax.experimental import pallas as pl
from jax.experimental.pallas import tpu as pltpu
from jax.sharding import PartitionSpec as P

MESH = pl.DeviceIdType.MESH
SEGMENT = 512
GROUPS = 8
PER_GROUP = 4
ROWS = 64
SLOTS = 5
WINDOW = ROWS * SLOTS
LANES = PER_GROUP * ROWS
WIDTH = 128
OWN = 4
AHEAD = 4
HIDDEN = -1e30
LOG2E = 1.4426950408889634


def kernel(
    q_hbm, k_hbm, v_hbm, g_hbm, span_hbm, off_hbm,
    attn_hbm, dq_hbm, dk_hbm, dv_hbm,
    qv, gv, kv, attn_v, dq_v, part, xs, xr, t2, ra, t1, rb, dkv, spans, offset,
    load_sem, hop1_s, hop1_r, hop2_s, hop2_r, pa_s, pa_r, pb_s, pb_r,
    x_s, x_r, a_s, a_r, b_s, b_r, out_sem, dkv_sem,
):
    core = lax.axis_index("head")
    here = lax.axis_index("seq")
    count = lax.axis_size("seq")
    after = {"seq": lax.rem(here + 1, count)}
    before = {"seq": lax.rem(here + count - 1, count)}
    partner = {"head": 1 - core}
    block = here * 2 + core
    scale = WIDTH ** -0.5

    barrier = pltpu.get_barrier_semaphore()
    for other in (after, before, partner):
        pl.semaphore_signal(barrier, inc=1, device_id=other, device_id_type=MESH)

    own_rows = pl.ds(OWN * ROWS, ROWS)
    loads = [
        pltpu.make_async_copy(k_hbm, kv.at[:, 0, own_rows, :], load_sem.at[0]),
        pltpu.make_async_copy(v_hbm, kv.at[:, 1, own_rows, :], load_sem.at[1]),
        pltpu.make_async_copy(q_hbm, qv, load_sem.at[2]),
        pltpu.make_async_copy(g_hbm, gv, load_sem.at[3]),
        pltpu.make_async_copy(span_hbm, spans, load_sem.at[4]),
        pltpu.make_async_copy(off_hbm, offset, load_sem.at[5]),
    ]
    for load in loads:
        load.start()
    xr[:, pl.ds(2 * core, 1)] = jnp.zeros((GROUPS, 1, 2, ROWS, WIDTH), jnp.bfloat16)

    def slot(g, s):
        return kv.at[g, :, pl.ds(pl.multiple_of(s * ROWS, ROWS), ROWS), :]

    def remote(src, dst, send, recv, other):
        return pltpu.make_async_remote_copy(
            src_ref=src, dst_ref=dst, send_sem=send, recv_sem=recv,
            device_id=other, device_id_type=MESH,
        )

    def hop1(g):
        return remote(slot(g, OWN), slot(g, 2), hop1_s.at[g], hop1_r.at[g], after)

    def hop2(g):
        return remote(slot(g, 2), slot(g, 0), hop2_s.at[g], hop2_r.at[g], after)

    def pair_near(g):
        return remote(slot(g, 4 - 2 * core), slot(g, 3), pa_s.at[g], pa_r.at[g], partner)

    def pair_far(g):
        return remote(slot(g, 2 - 2 * core), slot(g, 1), pb_s.at[g], pb_r.at[g], partner)

    def cross(g):
        return remote(xs.at[g], xr.at[g, pl.ds(core, 2)], x_s.at[g], x_r.at[g], partner)

    def cross_in(g):
        return remote(xs.at[g], xr.at[g, pl.ds(1 - core, 2)], x_s.at[g], x_r.at[g], partner)

    def chain2(g):
        return remote(t2.at[g], ra.at[g], a_s.at[g], a_r.at[g], before)

    def chain1(g):
        return remote(t1.at[g], rb.at[g], b_s.at[g], b_r.at[g], before)

    def heads(g):
        return pl.ds(pl.multiple_of(PER_GROUP * g, PER_GROUP), PER_GROUP)

    def attn_store(g):
        return pltpu.make_async_copy(attn_v.at[heads(g)], attn_hbm.at[heads(g)], out_sem.at[0, g])

    def dq_store(g):
        return pltpu.make_async_copy(dq_v.at[heads(g)], dq_hbm.at[heads(g)], out_sem.at[1, g])

    def dk_store(g):
        return pltpu.make_async_copy(dkv.at[g, 0], dk_hbm.at[g], dkv_sem.at[0, g])

    def dv_store(g):
        return pltpu.make_async_copy(dkv.at[g, 1], dv_hbm.at[g], dkv_sem.at[1, g])

    def on_hop1(g):
        hop1(g).wait_recv()
        hop2(g).start()

        @pl.when(g + AHEAD < GROUPS)
        def _():
            hop1(g + AHEAD).start()

        pair_near(g).start()

    def on_hop2(g):
        hop2(g).wait_recv()
        pair_far(g).start()

    lane = lax.broadcasted_iota(jnp.int32, (1, LANES), 1)
    row_in_block = lane & (ROWS - 1)
    query_row = row_in_block + OWN * ROWS

    def compute(g):
        pair_near(g).wait_recv()
        pair_far(g).wait_recv()
        span_of = [spans[PER_GROUP * g + a] for a in range(PER_GROUP)]
        span = jnp.where(
            lane < 2 * ROWS,
            jnp.where(lane < ROWS, span_of[0], span_of[1]),
            jnp.where(lane < 3 * ROWS, span_of[2], span_of[3]),
        )
        into_segment = (offset[0] + block * ROWS + row_in_block) & (SEGMENT - 1)
        lowest = query_row - jnp.minimum(span - 1, into_segment)
        lowest = jnp.maximum(lowest, (OWN - block) * ROWS)
        keys = kv[g, 0]
        values = kv[g, 1]
        queries = qv[heads(g)].reshape(LANES, WIDTH)
        grads = gv[heads(g)].reshape(LANES, WIDTH)
        last = (((1,), (1,)), ((), ()))
        first = (((0,), (0,)), ((), ()))
        scores = lax.dot_general(keys, queries, last, preferred_element_type=jnp.float32)
        prob_grad = lax.dot_general(values, grads, last, preferred_element_type=jnp.float32)
        key_row = lax.broadcasted_iota(jnp.int32, (WINDOW, LANES), 0)
        visible = (key_row >= lowest) & (key_row <= query_row)
        scores = jnp.where(visible, scores, HIDDEN)
        row_max = jnp.max(scores, axis=0, keepdims=True)
        weights = jnp.exp2((scores - row_max) * (scale * LOG2E))
        inverse = 1.0 / jnp.sum(weights, axis=0, keepdims=True)
        row_delta = jnp.sum(weights * prob_grad, axis=0, keepdims=True) * inverse
        attn = lax.dot_general(
            values, weights.astype(jnp.bfloat16), first, preferred_element_type=jnp.float32
        ) * inverse
        attn_v[heads(g)] = attn.T.astype(jnp.bfloat16).reshape(PER_GROUP, ROWS, WIDTH)
        attn_store(g).start()
        probs = (weights * inverse).astype(jnp.bfloat16)
        score_grad = (weights * ((prob_grad - row_delta) * (inverse * scale))).astype(jnp.bfloat16)
        dkey = jnp.dot(score_grad, queries, preferred_element_type=jnp.float32)
        dvalue = jnp.dot(probs, grads, preferred_element_type=jnp.float32)
        for j, s in enumerate((1, 3)):
            rows = slice(s * ROWS, (s + 1) * ROWS)
            xs[g, j, 0] = dkey[rows].astype(jnp.bfloat16)
            xs[g, j, 1] = dvalue[rows].astype(jnp.bfloat16)
        cross(g).start()
        for j, s in enumerate((0, 2, 4)):
            rows = slice(s * ROWS, (s + 1) * ROWS)
            part[g, j, 0] = dkey[rows]
            part[g, j, 1] = dvalue[rows]
        dquery = lax.dot_general(keys, score_grad, first, preferred_element_type=jnp.float32)
        dq_v[heads(g)] = dquery.T.astype(jnp.bfloat16).reshape(PER_GROUP, ROWS, WIDTH)
        dq_store(g).start()

    def on_cross(g):
        cross_in(g).wait_recv()
        t2[g] = (part[g, 0] + xr[g, 0].astype(jnp.float32)).astype(jnp.bfloat16)
        chain2(g).start()

    def on_chain2(g):
        chain2(g).wait_recv()
        total = part[g, 1] + xr[g, 1].astype(jnp.float32) + ra[g].astype(jnp.float32)
        t1[g] = total.astype(jnp.bfloat16)
        chain1(g).start()

    def on_chain1(g):
        chain1(g).wait_recv()
        total = part[g, 2] + xr[g, 2].astype(jnp.float32) + rb[g].astype(jnp.float32)
        dkv[g] = total.astype(jnp.bfloat16)
        dk_store(g).start()
        dv_store(g).start()

    loads[0].wait()
    loads[1].wait()
    pl.semaphore_wait(barrier, 3)
    for g in range(AHEAD):
        hop1(g).start()
    loads[2].wait()
    loads[3].wait()
    loads[4].wait()
    loads[5].wait()

    stages = ((on_hop1, 3), (on_hop2, 1), (compute, 0), (on_cross, -1), (on_chain2, -3), (on_chain1, -5))

    def turn(t, carry):
        for stage, lead in stages:
            g = t + lead

            @pl.when((g >= 0) & (g < GROUPS))
            def _(stage=stage, g=g):
                stage(g)

        return carry

    lax.fori_loop(-3, GROUPS + 5, turn, 0)

    def finish(g, carry):
        hop1(g).wait_send()
        hop2(g).wait_send()
        pair_near(g).wait_send()
        pair_far(g).wait_send()
        cross(g).wait_send()
        chain2(g).wait_send()
        chain1(g).wait_send()
        attn_store(g).wait()
        dq_store(g).wait()
        dk_store(g).wait()
        dv_store(g).wait()
        return carry

    lax.fori_loop(0, GROUPS, finish, 0)


def shards(query_matrix, key_matrix, value_matrix, output_gradient, query_head_spans, slab_offset):
    any_space = pl.BlockSpec(memory_space=pl.ANY)
    half = jnp.bfloat16
    group_sems = pltpu.SemaphoreType.DMA((GROUPS,))
    shapes = [
        jax.ShapeDtypeStruct(a.shape, a.dtype)
        for a in (query_matrix, query_matrix, key_matrix, value_matrix)
    ]
    return pl.pallas_call(
        kernel,
        out_shape=shapes,
        in_specs=[any_space] * 6,
        out_specs=[any_space] * 4,
        scratch_shapes=[
            pltpu.VMEM(query_matrix.shape, half),
            pltpu.VMEM(query_matrix.shape, half),
            pltpu.VMEM((GROUPS, 2, WINDOW, WIDTH), half),
            pltpu.VMEM(query_matrix.shape, half),
            pltpu.VMEM(query_matrix.shape, half),
            pltpu.VMEM((GROUPS, 3, 2, ROWS, WIDTH), jnp.float32),
            pltpu.VMEM((GROUPS, 2, 2, ROWS, WIDTH), half),
            pltpu.VMEM((GROUPS, 3, 2, ROWS, WIDTH), half),
            pltpu.VMEM((GROUPS, 2, ROWS, WIDTH), half),
            pltpu.VMEM((GROUPS, 2, ROWS, WIDTH), half),
            pltpu.VMEM((GROUPS, 2, ROWS, WIDTH), half),
            pltpu.VMEM((GROUPS, 2, ROWS, WIDTH), half),
            pltpu.VMEM((GROUPS, 2, ROWS, WIDTH), half),
            pltpu.SMEM((GROUPS * PER_GROUP,), jnp.int32),
            pltpu.SMEM((1,), jnp.int32),
            pltpu.SemaphoreType.DMA((6,)),
        ]
        + [group_sems] * 14
        + [pltpu.SemaphoreType.DMA((2, GROUPS))] * 2,
        compiler_params=pltpu.CompilerParams(collective_id=0, has_side_effects=True),
    )(query_matrix, key_matrix, value_matrix, output_gradient, query_head_spans, slab_offset)


def solution(mesh):
    blocks = P(None, ("seq", "head"), None)
    return jax.shard_map(
        shards,
        mesh=mesh,
        in_specs=(blocks, blocks, blocks, blocks, P(), P()),
        out_specs=(blocks, blocks, blocks, blocks),
        check_vma=False,
    )
```

```python
import jax
import jax.numpy as jnp
from jax import lax
from jax.experimental import pallas as pl
from jax.experimental.pallas import tpu as pltpu
from jax.sharding import PartitionSpec as P

MESH = pl.DeviceIdType.MESH
SEGMENT = 512
GROUPS = 8
PER_GROUP = 4
ROWS = 64
SLOTS = 5
WINDOW = ROWS * SLOTS
LANES = PER_GROUP * ROWS
WIDTH = 128
OWN = 4
AHEAD = 8
DIRECT_KEYS = 8
DIRECT_GRADS = 8
LEADS = (3, 1, -1, -2, -4)
HIDDEN = -1e30
LOG2E = 1.4426950408889634


def kernel(
    q_hbm, k_hbm, v_hbm, g_hbm, span_hbm, off_hbm,
    attn_v, dq_v, dk_v, dv_v,
    qv, gv, kv, part, xs, xr, t2, ra, t1, rb, spans, offset,
    load_sem, hop1_s, hop1_r, hop2_s, hop2_r, pa_s, pa_r, pb_s, pb_r,
    x_s, x_r, a_s, a_r, b_s, b_r,
):
    core = lax.axis_index("head")
    here = lax.axis_index("seq")
    count = lax.axis_size("seq")
    after = {"seq": lax.rem(here + 1, count)}
    before = {"seq": lax.rem(here + count - 1, count)}
    after2 = {"seq": lax.rem(here + 2, count)}
    before2 = {"seq": lax.rem(here + count - 2, count)}
    partner = {"head": 1 - core}
    block = here * 2 + core
    scale = WIDTH ** -0.5

    barrier = pltpu.get_barrier_semaphore()
    has_before = here >= 1
    has_after = here < count - 1
    two_before = here >= 2
    two_after = here < count - 2

    def greet(other):
        pl.semaphore_signal(barrier, inc=1, device_id=other, device_id_type=MESH)

    greet(partner)
    pl.when(has_before)(lambda: greet(before))
    pl.when(has_after)(lambda: greet(after))
    pl.when(two_before)(lambda: greet(before2))
    pl.when(two_after)(lambda: greet(after2))

    own_rows = pl.ds(OWN * ROWS, ROWS)
    loads = [
        pltpu.make_async_copy(k_hbm, kv.at[:, 0, own_rows, :], load_sem.at[0]),
        pltpu.make_async_copy(v_hbm, kv.at[:, 1, own_rows, :], load_sem.at[1]),
        pltpu.make_async_copy(q_hbm, qv, load_sem.at[2]),
        pltpu.make_async_copy(g_hbm, gv, load_sem.at[3]),
        pltpu.make_async_copy(span_hbm, spans, load_sem.at[4]),
        pltpu.make_async_copy(off_hbm, offset, load_sem.at[5]),
    ]
    for load in loads:
        load.start()

    def clear(ref):
        ref[...] = jnp.zeros(ref.shape, ref.dtype)

    pl.when(jnp.logical_not(two_before))(lambda: clear(kv.at[:, :, pl.ds(0, ROWS), :]))
    pl.when(jnp.logical_not(has_before))(lambda: clear(kv.at[:, :, pl.ds(2 * ROWS, ROWS), :]))
    pl.when(jnp.logical_not(has_after))(lambda: clear(ra))
    if DIRECT_GRADS:
        direct_part = ra.at[pl.ds(GROUPS - DIRECT_GRADS, DIRECT_GRADS)]
        pl.when(has_after & jnp.logical_not(two_after))(lambda: clear(direct_part))
    pl.when(jnp.logical_not(has_after))(lambda: clear(rb))
    xr[:, pl.ds(2 * core, 1)] = jnp.zeros((GROUPS, 1, 2, ROWS, WIDTH), jnp.bfloat16)

    def slot(g, s):
        return kv.at[g, :, pl.ds(pl.multiple_of(s * ROWS, ROWS), ROWS), :]

    def remote(src, dst, send, recv, other):
        return pltpu.make_async_remote_copy(
            src_ref=src, dst_ref=dst, send_sem=send, recv_sem=recv,
            device_id=other, device_id_type=MESH,
        )

    def hop1(g):
        return remote(slot(g, OWN), slot(g, 2), hop1_s.at[g], hop1_r.at[g], after)

    def hop2(g):
        return remote(slot(g, 2), slot(g, 0), hop2_s.at[g], hop2_r.at[g], after)

    def hop2_direct(g):
        return remote(slot(g, OWN), slot(g, 0), hop2_s.at[g], hop2_r.at[g], after2)

    def pair_near(g):
        return remote(slot(g, 4 - 2 * core), slot(g, 3), pa_s.at[g], pa_r.at[g], partner)

    def pair_far(g):
        return remote(slot(g, 2 - 2 * core), slot(g, 1), pb_s.at[g], pb_r.at[g], partner)

    def cross(g):
        return remote(xs.at[g], xr.at[g, pl.ds(core, 2)], x_s.at[g], x_r.at[g], partner)

    def cross_in(g):
        return remote(xs.at[g], xr.at[g, pl.ds(1 - core, 2)], x_s.at[g], x_r.at[g], partner)

    def chain2(g):
        return remote(t2.at[g], ra.at[g], a_s.at[g], a_r.at[g], before)

    def chain2_direct(g):
        return remote(t2.at[g], ra.at[g], a_s.at[g], a_r.at[g], before2)

    def chain1(g):
        return remote(t1.at[g], rb.at[g], b_s.at[g], b_r.at[g], before)

    def heads(g):
        return pl.ds(pl.multiple_of(PER_GROUP * g, PER_GROUP), PER_GROUP)

    def on_hop1(g):
        @pl.when(has_before)
        def _():
            hop1(g).wait_recv()
            pl.when(has_after & (g >= DIRECT_KEYS))(lambda: hop2(g).start())

        @pl.when(has_after & (g + AHEAD < GROUPS))
        def _():
            hop1(g + AHEAD).start()

        pair_near(g).start()

    def on_hop2(g):
        pl.when(two_before)(lambda: hop2(g).wait_recv())
        pair_far(g).start()

    lane = lax.broadcasted_iota(jnp.int32, (1, LANES), 1)
    row_in_block = lane & (ROWS - 1)
    query_row = row_in_block + OWN * ROWS

    def compute(g):
        pair_near(g).wait_recv()
        pair_far(g).wait_recv()
        span_of = [spans[PER_GROUP * g + a] for a in range(PER_GROUP)]
        span = jnp.where(
            lane < 2 * ROWS,
            jnp.where(lane < ROWS, span_of[0], span_of[1]),
            jnp.where(lane < 3 * ROWS, span_of[2], span_of[3]),
        )
        into_segment = (offset[0] + block * ROWS + row_in_block) & (SEGMENT - 1)
        lowest = query_row - jnp.minimum(span - 1, into_segment)
        lowest = jnp.maximum(lowest, (OWN - block) * ROWS)
        keys = kv[g, 0]
        values = kv[g, 1]
        queries = qv[heads(g)].reshape(LANES, WIDTH)
        grads = gv[heads(g)].reshape(LANES, WIDTH)
        last = (((1,), (1,)), ((), ()))
        first = (((0,), (0,)), ((), ()))
        scores = lax.dot_general(keys, queries, last, preferred_element_type=jnp.float32)
        prob_grad = lax.dot_general(values, grads, last, preferred_element_type=jnp.float32)
        key_row = lax.broadcasted_iota(jnp.int32, (WINDOW, LANES), 0)
        visible = (key_row >= lowest) & (key_row <= query_row)
        scores = jnp.where(visible, scores, HIDDEN)
        row_max = jnp.max(scores, axis=0, keepdims=True)
        weights = jnp.exp2((scores - row_max) * (scale * LOG2E))
        inverse = 1.0 / jnp.sum(weights, axis=0, keepdims=True)
        row_delta = jnp.sum(weights * prob_grad, axis=0, keepdims=True) * inverse
        attn = lax.dot_general(
            values, weights.astype(jnp.bfloat16), first, preferred_element_type=jnp.float32
        ) * inverse
        attn_v[heads(g)] = attn.T.astype(jnp.bfloat16).reshape(PER_GROUP, ROWS, WIDTH)
        probs = (weights * inverse).astype(jnp.bfloat16)
        score_grad = (weights * ((prob_grad - row_delta) * (inverse * scale))).astype(jnp.bfloat16)
        dkey = jnp.dot(score_grad, queries, preferred_element_type=jnp.float32)
        dvalue = jnp.dot(probs, grads, preferred_element_type=jnp.float32)
        for j, s in enumerate((1, 3)):
            rows = slice(s * ROWS, (s + 1) * ROWS)
            xs[g, j, 0] = dkey[rows].astype(jnp.bfloat16)
            xs[g, j, 1] = dvalue[rows].astype(jnp.bfloat16)
        cross(g).start()
        for j, s in enumerate((0, 2, 4)):
            rows = slice(s * ROWS, (s + 1) * ROWS)
            part[g, j, 0] = dkey[rows]
            part[g, j, 1] = dvalue[rows]
        dquery = lax.dot_general(keys, score_grad, first, preferred_element_type=jnp.float32)
        dq_v[heads(g)] = dquery.T.astype(jnp.bfloat16).reshape(PER_GROUP, ROWS, WIDTH)

    def send_t1(g, total):
        t1[g] = total.astype(jnp.bfloat16)
        chain1(g).start()

    def on_cross(g):
        cross_in(g).wait_recv()
        direct = g >= GROUPS - DIRECT_GRADS

        @pl.when(two_before)
        def _():
            t2[g] = (part[g, 0] + xr[g, 0].astype(jnp.float32)).astype(jnp.bfloat16)
            pl.when(direct)(lambda: chain2_direct(g).start())
            pl.when(jnp.logical_not(direct))(lambda: chain2(g).start())

        @pl.when(has_before & direct)
        def _():
            send_t1(g, part[g, 1] + xr[g, 1].astype(jnp.float32))

    def on_chain2(g):
        @pl.when(has_before & (g < GROUPS - DIRECT_GRADS))
        def _():
            pl.when(has_after)(lambda: chain2(g).wait_recv())
            send_t1(g, part[g, 1] + xr[g, 1].astype(jnp.float32) + ra[g].astype(jnp.float32))

    def on_chain1(g):
        direct = g >= GROUPS - DIRECT_GRADS
        pl.when(has_after)(lambda: chain1(g).wait_recv())
        pl.when(two_after & direct)(lambda: chain2_direct(g).wait_recv())
        total = part[g, 2] + xr[g, 2].astype(jnp.float32) + rb[g].astype(jnp.float32)
        extra = ra[g].astype(jnp.float32)
        total = total + jnp.where(direct, extra, jnp.zeros_like(extra))
        dk_v[g] = total[0].astype(jnp.bfloat16)
        dv_v[g] = total[1].astype(jnp.bfloat16)

    loads[0].wait()
    loads[1].wait()
    pl.semaphore_wait(barrier, 1 + jnp.minimum(here, 2) + jnp.minimum(count - 1 - here, 2))

    for g in range(AHEAD):
        pl.when(has_after)(lambda g=g: hop1(g).start())
        if g < DIRECT_KEYS:
            pl.when(two_after)(lambda g=g: hop2_direct(g).start())

    loads[2].wait()
    loads[3].wait()
    loads[4].wait()
    loads[5].wait()

    works = (on_hop1, on_hop2, compute, on_cross, on_chain2, on_chain1)
    stages = tuple(zip(works, LEADS[:2] + (0,) + LEADS[2:]))

    def turn(t, carry):
        for stage, lead in stages:
            g = t + lead

            @pl.when((g >= 0) & (g < GROUPS))
            def _(stage=stage, g=g):
                stage(g)

        return carry

    lax.fori_loop(-LEADS[0], GROUPS - LEADS[-1], turn, 0)

    def finish(g, carry):
        pl.when(has_after)(lambda: hop1(g).wait_send())
        relayed = g >= DIRECT_KEYS
        pl.when((relayed & has_before & has_after) | (jnp.logical_not(relayed) & two_after))(
            lambda: hop2(g).wait_send()
        )
        pair_near(g).wait_send()
        pair_far(g).wait_send()
        cross(g).wait_send()
        pl.when(two_before)(lambda: chain2(g).wait_send())
        pl.when(has_before)(lambda: chain1(g).wait_send())
        return carry

    lax.fori_loop(0, GROUPS, finish, 0)


def flush(*refs):
    copies = [
        pltpu.make_async_copy(refs[i], refs[4 + i], refs[8].at[i]) for i in range(4)
    ]
    for copy in copies:
        copy.start()
    for copy in copies:
        copy.wait()


def shards(query_matrix, key_matrix, value_matrix, output_gradient, query_head_spans, slab_offset):
    any_space = pl.BlockSpec(memory_space=pl.ANY)
    vmem_space = pl.BlockSpec(memory_space=pltpu.VMEM)
    half = jnp.bfloat16
    group_sems = pltpu.SemaphoreType.DMA((GROUPS,))
    shapes = [
        jax.ShapeDtypeStruct(a.shape, a.dtype)
        for a in (query_matrix, query_matrix, key_matrix, value_matrix)
    ]
    results = pl.pallas_call(
        kernel,
        out_shape=[pltpu.VMEM(a.shape, a.dtype) for a in shapes],
        in_specs=[any_space] * 6,
        out_specs=[vmem_space] * 4,
        scratch_shapes=[
            pltpu.VMEM(query_matrix.shape, half),
            pltpu.VMEM(query_matrix.shape, half),
            pltpu.VMEM((GROUPS, 2, WINDOW, WIDTH), half),
            pltpu.VMEM((GROUPS, 3, 2, ROWS, WIDTH), jnp.float32),
            pltpu.VMEM((GROUPS, 2, 2, ROWS, WIDTH), half),
            pltpu.VMEM((GROUPS, 3, 2, ROWS, WIDTH), half),
            pltpu.VMEM((GROUPS, 2, ROWS, WIDTH), half),
            pltpu.VMEM((GROUPS, 2, ROWS, WIDTH), half),
            pltpu.VMEM((GROUPS, 2, ROWS, WIDTH), half),
            pltpu.VMEM((GROUPS, 2, ROWS, WIDTH), half),
            pltpu.SMEM((GROUPS * PER_GROUP,), jnp.int32),
            pltpu.SMEM((1,), jnp.int32),
            pltpu.SemaphoreType.DMA((6,)),
        ]
        + [group_sems] * 14,
        compiler_params=pltpu.CompilerParams(collective_id=0, has_side_effects=True),
    )(query_matrix, key_matrix, value_matrix, output_gradient, query_head_spans, slab_offset)
    return pl.pallas_call(
        flush,
        out_shape=shapes,
        in_specs=[vmem_space] * 4,
        out_specs=[any_space] * 4,
        scratch_shapes=[pltpu.SemaphoreType.DMA((4,))],
    )(*[pltpu.with_memory_space_constraint(r, pltpu.VMEM) for r in results])


def solution(mesh):
    blocks = P(None, ("seq", "head"), None)
    return jax.shard_map(
        shards,
        mesh=mesh,
        in_specs=(blocks, blocks, blocks, blocks, P(), P()),
        out_specs=(blocks, blocks, blocks, blocks),
        check_vma=False,
    )
```

```python
import jax
import jax.numpy as jnp
from jax import lax
from jax.experimental import pallas as pl
from jax.experimental.pallas import tpu as pltpu
from jax.sharding import PartitionSpec as P

MESH = pl.DeviceIdType.MESH
SEGMENT = 512
GROUPS = 8
PER_GROUP = 4
ROWS = 64
SLOTS = 5
WINDOW = ROWS * SLOTS
LANES = PER_GROUP * ROWS
WIDTH = 128
OWN = 4
AHEAD = 8
DIRECT_KEYS = 8
DIRECT_GRADS = 8
LEADS = (1, 1, -1, -2, -8)
HIDDEN = -1e30
LOG2E = 1.4426950408889634


def kernel(
    q_hbm, k_hbm, v_hbm, g_hbm, span_hbm, off_hbm,
    attn_v, dq_v, dk_v, dv_v,
    qv, gv, kv, part, xs, xr, t2, ra, t1, rb, spans, offset,
    load_sem, hop1_s, hop1_r, hop2_s, hop2_r, pa_s, pa_r, pb_s, pb_r,
    x_s, x_r, a_s, a_r, b_s, b_r,
):
    core = lax.axis_index("head")
    here = lax.axis_index("seq")
    count = lax.axis_size("seq")
    after = {"seq": lax.rem(here + 1, count)}
    before = {"seq": lax.rem(here + count - 1, count)}
    after2 = {"seq": lax.rem(here + 2, count)}
    before2 = {"seq": lax.rem(here + count - 2, count)}
    partner = {"head": 1 - core}
    block = here * 2 + core
    scale = WIDTH ** -0.5

    barrier = pltpu.get_barrier_semaphore()
    has_before = here >= 1
    has_after = here < count - 1
    two_before = here >= 2
    two_after = here < count - 2

    def greet(other):
        pl.semaphore_signal(barrier, inc=1, device_id=other, device_id_type=MESH)

    greet(partner)
    pl.when(has_before)(lambda: greet(before))
    pl.when(has_after)(lambda: greet(after))
    pl.when(two_before)(lambda: greet(before2))
    pl.when(two_after)(lambda: greet(after2))

    own_rows = pl.ds(OWN * ROWS, ROWS)
    loads = [
        pltpu.make_async_copy(k_hbm, kv.at[:, 0, own_rows, :], load_sem.at[0]),
        pltpu.make_async_copy(v_hbm, kv.at[:, 1, own_rows, :], load_sem.at[1]),
        pltpu.make_async_copy(q_hbm, qv, load_sem.at[2]),
        pltpu.make_async_copy(g_hbm, gv, load_sem.at[3]),
        pltpu.make_async_copy(span_hbm, spans, load_sem.at[4]),
        pltpu.make_async_copy(off_hbm, offset, load_sem.at[5]),
    ]
    for load in loads:
        load.start()

    def clear(ref):
        ref[...] = jnp.zeros(ref.shape, ref.dtype)

    pl.when(jnp.logical_not(two_before))(lambda: clear(kv.at[:, :, pl.ds(0, ROWS), :]))
    pl.when(jnp.logical_not(has_before))(lambda: clear(kv.at[:, :, pl.ds(2 * ROWS, ROWS), :]))
    pl.when(jnp.logical_not(has_after))(lambda: clear(ra))
    if DIRECT_GRADS:
        direct_part = ra.at[pl.ds(GROUPS - DIRECT_GRADS, DIRECT_GRADS)]
        pl.when(has_after & jnp.logical_not(two_after))(lambda: clear(direct_part))
    pl.when(jnp.logical_not(has_after))(lambda: clear(rb))
    xr[:, pl.ds(2 * core, 1)] = jnp.zeros((GROUPS, 1, 2, ROWS, WIDTH), jnp.bfloat16)

    def slot(g, s):
        return kv.at[g, :, pl.ds(pl.multiple_of(s * ROWS, ROWS), ROWS), :]

    def remote(src, dst, send, recv, other):
        return pltpu.make_async_remote_copy(
            src_ref=src, dst_ref=dst, send_sem=send, recv_sem=recv,
            device_id=other, device_id_type=MESH,
        )

    def hop1(g):
        return remote(slot(g, OWN), slot(g, 2), hop1_s.at[g], hop1_r.at[g], after)

    def hop2(g):
        return remote(slot(g, 2), slot(g, 0), hop2_s.at[g], hop2_r.at[g], after)

    def hop2_direct(g):
        return remote(slot(g, OWN), slot(g, 0), hop2_s.at[g], hop2_r.at[g], after2)

    def pair_near(g):
        return remote(slot(g, 4 - 2 * core), slot(g, 3), pa_s.at[g], pa_r.at[g], partner)

    def pair_far(g):
        return remote(slot(g, 2 - 2 * core), slot(g, 1), pb_s.at[g], pb_r.at[g], partner)

    def cross(g):
        return remote(xs.at[g], xr.at[g, pl.ds(core, 2)], x_s.at[g], x_r.at[g], partner)

    def cross_in(g):
        return remote(xs.at[g], xr.at[g, pl.ds(1 - core, 2)], x_s.at[g], x_r.at[g], partner)

    def chain2(g):
        return remote(t2.at[g], ra.at[g], a_s.at[g], a_r.at[g], before)

    def chain2_direct(g):
        return remote(t2.at[g], ra.at[g], a_s.at[g], a_r.at[g], before2)

    def chain1(g):
        return remote(t1.at[g], rb.at[g], b_s.at[g], b_r.at[g], before)

    def heads(g):
        return pl.ds(pl.multiple_of(PER_GROUP * g, PER_GROUP), PER_GROUP)

    def on_hop1(g):
        @pl.when(has_before)
        def _():
            hop1(g).wait_recv()
            pl.when(has_after & (g >= DIRECT_KEYS))(lambda: hop2(g).start())

        @pl.when(has_after & (g + AHEAD < GROUPS))
        def _():
            hop1(g + AHEAD).start()

        pair_near(g).start()

    def on_hop2(g):
        pl.when(two_before)(lambda: hop2(g).wait_recv())
        pair_far(g).start()

    lane = lax.broadcasted_iota(jnp.int32, (1, LANES), 1)
    row_in_block = lane & (ROWS - 1)
    query_row = row_in_block + OWN * ROWS

    def compute(g):
        pair_near(g).wait_recv()
        pair_far(g).wait_recv()
        span_of = [spans[PER_GROUP * g + a] for a in range(PER_GROUP)]
        span = jnp.where(
            lane < 2 * ROWS,
            jnp.where(lane < ROWS, span_of[0], span_of[1]),
            jnp.where(lane < 3 * ROWS, span_of[2], span_of[3]),
        )
        into_segment = (offset[0] + block * ROWS + row_in_block) & (SEGMENT - 1)
        lowest = query_row - jnp.minimum(span - 1, into_segment)
        lowest = jnp.maximum(lowest, (OWN - block) * ROWS)
        keys = kv[g, 0]
        values = kv[g, 1]
        queries = qv[heads(g)].reshape(LANES, WIDTH)
        grads = gv[heads(g)].reshape(LANES, WIDTH)
        last = (((1,), (1,)), ((), ()))
        first = (((0,), (0,)), ((), ()))
        scores = lax.dot_general(keys, queries, last, preferred_element_type=jnp.float32)
        prob_grad = lax.dot_general(values, grads, last, preferred_element_type=jnp.float32)
        key_row = lax.broadcasted_iota(jnp.int32, (WINDOW, LANES), 0)
        visible = (key_row >= lowest) & (key_row <= query_row)
        scores = jnp.where(visible, scores, HIDDEN)
        row_max = jnp.max(scores, axis=0, keepdims=True)
        weights = jnp.exp2((scores - row_max) * (scale * LOG2E))
        inverse = 1.0 / jnp.sum(weights, axis=0, keepdims=True)
        row_delta = jnp.sum(weights * prob_grad, axis=0, keepdims=True) * inverse
        probs = (weights * inverse).astype(jnp.bfloat16)
        score_grad = (weights * ((prob_grad - row_delta) * (inverse * scale))).astype(jnp.bfloat16)
        dkey = jnp.dot(score_grad, queries, preferred_element_type=jnp.float32)
        dvalue = jnp.dot(probs, grads, preferred_element_type=jnp.float32)
        for j, s in enumerate((1, 3)):
            rows = slice(s * ROWS, (s + 1) * ROWS)
            xs[g, j, 0] = dkey[rows].astype(jnp.bfloat16)
            xs[g, j, 1] = dvalue[rows].astype(jnp.bfloat16)
        cross(g).start()
        for j, s in enumerate((0, 2, 4)):
            rows = slice(s * ROWS, (s + 1) * ROWS)
            part[g, j, 0] = dkey[rows]
            part[g, j, 1] = dvalue[rows]
        attn = lax.dot_general(
            values, weights.astype(jnp.bfloat16), first, preferred_element_type=jnp.float32
        ) * inverse
        attn_v[heads(g)] = attn.T.astype(jnp.bfloat16).reshape(PER_GROUP, ROWS, WIDTH)
        dquery = lax.dot_general(keys, score_grad, first, preferred_element_type=jnp.float32)
        dq_v[heads(g)] = dquery.T.astype(jnp.bfloat16).reshape(PER_GROUP, ROWS, WIDTH)

    def send_t1(g, total):
        t1[g] = total.astype(jnp.bfloat16)
        chain1(g).start()

    def on_cross(g):
        cross_in(g).wait_recv()
        direct = g >= GROUPS - DIRECT_GRADS

        @pl.when(two_before)
        def _():
            t2[g] = (part[g, 0] + xr[g, 0].astype(jnp.float32)).astype(jnp.bfloat16)
            pl.when(direct)(lambda: chain2_direct(g).start())
            pl.when(jnp.logical_not(direct))(lambda: chain2(g).start())

        @pl.when(has_before & direct)
        def _():
            send_t1(g, part[g, 1] + xr[g, 1].astype(jnp.float32))

    def on_chain2(g):
        @pl.when(has_before & (g < GROUPS - DIRECT_GRADS))
        def _():
            pl.when(has_after)(lambda: chain2(g).wait_recv())
            send_t1(g, part[g, 1] + xr[g, 1].astype(jnp.float32) + ra[g].astype(jnp.float32))

    def on_chain1(g):
        direct = g >= GROUPS - DIRECT_GRADS
        pl.when(has_after)(lambda: chain1(g).wait_recv())
        pl.when(two_after & direct)(lambda: chain2_direct(g).wait_recv())
        total = part[g, 2] + xr[g, 2].astype(jnp.float32) + rb[g].astype(jnp.float32)
        extra = ra[g].astype(jnp.float32)
        total = total + jnp.where(direct, extra, jnp.zeros_like(extra))
        dk_v[g] = total[0].astype(jnp.bfloat16)
        dv_v[g] = total[1].astype(jnp.bfloat16)

    loads[0].wait()
    loads[1].wait()
    pl.semaphore_wait(barrier, 1 + jnp.minimum(here, 2) + jnp.minimum(count - 1 - here, 2))

    for g in range(AHEAD):
        pl.when(has_after)(lambda g=g: hop1(g).start())
        if g < DIRECT_KEYS:
            pl.when(two_after)(lambda g=g: hop2_direct(g).start())

    loads[2].wait()
    loads[3].wait()
    loads[4].wait()
    loads[5].wait()

    works = (on_hop1, on_hop2, compute, on_cross, on_chain2, on_chain1)
    stages = tuple(zip(works, LEADS[:2] + (0,) + LEADS[2:]))

    def turn(t, carry):
        for stage, lead in stages:
            g = t + lead

            @pl.when((g >= 0) & (g < GROUPS))
            def _(stage=stage, g=g):
                stage(g)

        return carry

    lax.fori_loop(-LEADS[0], GROUPS - LEADS[-1], turn, 0)

    def finish(g, carry):
        pl.when(has_after)(lambda: hop1(g).wait_send())
        relayed = g >= DIRECT_KEYS
        pl.when((relayed & has_before & has_after) | (jnp.logical_not(relayed) & two_after))(
            lambda: hop2(g).wait_send()
        )
        pair_near(g).wait_send()
        pair_far(g).wait_send()
        cross(g).wait_send()
        pl.when(two_before)(lambda: chain2(g).wait_send())
        pl.when(has_before)(lambda: chain1(g).wait_send())
        return carry

    lax.fori_loop(0, GROUPS, finish, 0)


def flush(*refs):
    copies = [
        pltpu.make_async_copy(refs[i], refs[4 + i], refs[8].at[i]) for i in range(4)
    ]
    for copy in copies:
        copy.start()
    for copy in copies:
        copy.wait()


def shards(query_matrix, key_matrix, value_matrix, output_gradient, query_head_spans, slab_offset):
    any_space = pl.BlockSpec(memory_space=pl.ANY)
    vmem_space = pl.BlockSpec(memory_space=pltpu.VMEM)
    half = jnp.bfloat16
    group_sems = pltpu.SemaphoreType.DMA((GROUPS,))
    shapes = [
        jax.ShapeDtypeStruct(a.shape, a.dtype)
        for a in (query_matrix, query_matrix, key_matrix, value_matrix)
    ]
    results = pl.pallas_call(
        kernel,
        out_shape=[pltpu.VMEM(a.shape, a.dtype) for a in shapes],
        in_specs=[any_space] * 6,
        out_specs=[vmem_space] * 4,
        scratch_shapes=[
            pltpu.VMEM(query_matrix.shape, half),
            pltpu.VMEM(query_matrix.shape, half),
            pltpu.VMEM((GROUPS, 2, WINDOW, WIDTH), half),
            pltpu.VMEM((GROUPS, 3, 2, ROWS, WIDTH), jnp.float32),
            pltpu.VMEM((GROUPS, 2, 2, ROWS, WIDTH), half),
            pltpu.VMEM((GROUPS, 3, 2, ROWS, WIDTH), half),
            pltpu.VMEM((GROUPS, 2, ROWS, WIDTH), half),
            pltpu.VMEM((GROUPS, 2, ROWS, WIDTH), half),
            pltpu.VMEM((GROUPS, 2, ROWS, WIDTH), half),
            pltpu.VMEM((GROUPS, 2, ROWS, WIDTH), half),
            pltpu.SMEM((GROUPS * PER_GROUP,), jnp.int32),
            pltpu.SMEM((1,), jnp.int32),
            pltpu.SemaphoreType.DMA((6,)),
        ]
        + [group_sems] * 14,
        compiler_params=pltpu.CompilerParams(collective_id=0, has_side_effects=True),
    )(query_matrix, key_matrix, value_matrix, output_gradient, query_head_spans, slab_offset)
    return pl.pallas_call(
        flush,
        out_shape=shapes,
        in_specs=[vmem_space] * 4,
        out_specs=[any_space] * 4,
        scratch_shapes=[pltpu.SemaphoreType.DMA((4,))],
    )(*[pltpu.with_memory_space_constraint(r, pltpu.VMEM) for r in results])


def solution(mesh):
    blocks = P(None, ("seq", "head"), None)
    return jax.shard_map(
        shards,
        mesh=mesh,
        in_specs=(blocks, blocks, blocks, blocks, P(), P()),
        out_specs=(blocks, blocks, blocks, blocks),
        check_vma=False,
    )
```

```python
import jax
import jax.numpy as jnp
from jax import lax
from jax.experimental import pallas as pl
from jax.experimental.pallas import tpu as pltpu
from jax.sharding import PartitionSpec as P

MESH = pl.DeviceIdType.MESH
SEGMENT = 512
GROUPS = 8
PER_GROUP = 4
ROWS = 64
SLOTS = 5
WINDOW = ROWS * SLOTS
LANES = PER_GROUP * ROWS
WIDTH = 128
OWN = 4
AHEAD = 8
DIRECT_KEYS = 8
DIRECT_GRADS = 8
LEADS = (1, 1, -1, -2, -8)
HIDDEN = -1e30
LOG2E = 1.4426950408889634


def kernel(
    q_hbm, k_hbm, v_hbm, g_hbm, span_hbm, off_hbm,
    attn_v, dq_v, dk_v, dv_v,
    qv, gv, kv, part, xs, xr, t2, ra, t1, rb, spans, offset,
    load_sem, hop1_s, hop1_r, hop2_s, hop2_r, pa_s, pa_r, pb_s, pb_r,
    x_s, x_r, a_s, a_r, b_s, b_r,
):
    core = lax.axis_index("head")
    here = lax.axis_index("seq")
    count = lax.axis_size("seq")
    after = {"seq": lax.rem(here + 1, count)}
    before = {"seq": lax.rem(here + count - 1, count)}
    after2 = {"seq": lax.rem(here + 2, count)}
    before2 = {"seq": lax.rem(here + count - 2, count)}
    partner = {"head": 1 - core}
    block = here * 2 + core
    scale = WIDTH ** -0.5

    barrier = pltpu.get_barrier_semaphore()
    has_before = here >= 1
    has_after = here < count - 1
    two_before = here >= 2
    two_after = here < count - 2

    def greet(other):
        pl.semaphore_signal(barrier, inc=1, device_id=other, device_id_type=MESH)

    greet(partner)
    pl.when(has_before)(lambda: greet(before))
    pl.when(has_after)(lambda: greet(after))
    pl.when(two_before)(lambda: greet(before2))
    pl.when(two_after)(lambda: greet(after2))

    own_rows = pl.ds(OWN * ROWS, ROWS)
    loads = [
        pltpu.make_async_copy(k_hbm, kv.at[:, 0, own_rows, :], load_sem.at[0]),
        pltpu.make_async_copy(v_hbm, kv.at[:, 1, own_rows, :], load_sem.at[1]),
        pltpu.make_async_copy(q_hbm, qv, load_sem.at[2]),
        pltpu.make_async_copy(g_hbm, gv, load_sem.at[3]),
        pltpu.make_async_copy(span_hbm, spans, load_sem.at[4]),
        pltpu.make_async_copy(off_hbm, offset, load_sem.at[5]),
    ]
    for load in loads:
        load.start()

    def clear(ref):
        ref[...] = jnp.zeros(ref.shape, ref.dtype)

    pl.when(jnp.logical_not(two_before))(lambda: clear(kv.at[:, :, pl.ds(0, ROWS), :]))
    pl.when(jnp.logical_not(has_before))(lambda: clear(kv.at[:, :, pl.ds(2 * ROWS, ROWS), :]))
    pl.when(jnp.logical_not(has_after))(lambda: clear(ra))
    if DIRECT_GRADS:
        direct_part = ra.at[pl.ds(GROUPS - DIRECT_GRADS, DIRECT_GRADS)]
        pl.when(has_after & jnp.logical_not(two_after))(lambda: clear(direct_part))
    pl.when(jnp.logical_not(has_after))(lambda: clear(rb))
    xr[:, pl.ds(2 * core, 1)] = jnp.zeros((GROUPS, 1, 2, ROWS, WIDTH), jnp.bfloat16)

    def slot(g, s):
        return kv.at[g, :, pl.ds(pl.multiple_of(s * ROWS, ROWS), ROWS), :]

    def remote(src, dst, send, recv, other):
        return pltpu.make_async_remote_copy(
            src_ref=src, dst_ref=dst, send_sem=send, recv_sem=recv,
            device_id=other, device_id_type=MESH,
        )

    def hop1(g):
        return remote(slot(g, OWN), slot(g, 2), hop1_s.at[g], hop1_r.at[g], after)

    def hop2(g):
        return remote(slot(g, 2), slot(g, 0), hop2_s.at[g], hop2_r.at[g], after)

    def hop2_direct(g):
        return remote(slot(g, OWN), slot(g, 0), hop2_s.at[g], hop2_r.at[g], after2)

    def pair_near(g):
        return remote(slot(g, 4 - 2 * core), slot(g, 3), pa_s.at[g], pa_r.at[g], partner)

    def pair_far(g):
        return remote(slot(g, 2 - 2 * core), slot(g, 1), pb_s.at[g], pb_r.at[g], partner)

    def cross(g):
        return remote(xs.at[g], xr.at[g, pl.ds(core, 2)], x_s.at[g], x_r.at[g], partner)

    def cross_in(g):
        return remote(xs.at[g], xr.at[g, pl.ds(1 - core, 2)], x_s.at[g], x_r.at[g], partner)

    def chain2(g):
        return remote(t2.at[g], ra.at[g], a_s.at[g], a_r.at[g], before)

    def chain2_direct(g):
        return remote(t2.at[g], ra.at[g], a_s.at[g], a_r.at[g], before2)

    def chain1(g):
        return remote(t1.at[g], rb.at[g], b_s.at[g], b_r.at[g], before)

    def heads(g):
        return pl.ds(pl.multiple_of(PER_GROUP * g, PER_GROUP), PER_GROUP)

    def on_hop1(g):
        @pl.when(has_before)
        def _():
            hop1(g).wait_recv()
            pl.when(has_after & (g >= DIRECT_KEYS))(lambda: hop2(g).start())

        @pl.when(has_after & (g + AHEAD < GROUPS))
        def _():
            hop1(g + AHEAD).start()

        pair_near(g).start()

    def on_hop2(g):
        pl.when(two_before)(lambda: hop2(g).wait_recv())
        pair_far(g).start()

    lane = lax.broadcasted_iota(jnp.int32, (1, LANES), 1)
    row_in_block = lane & (ROWS - 1)
    query_row = row_in_block + OWN * ROWS

    def compute(g):
        @pl.when(g == 0)
        def _():
            for load in loads[2:]:
                load.wait()

        pair_near(g).wait_recv()
        pair_far(g).wait_recv()
        span_of = [spans[PER_GROUP * g + a] for a in range(PER_GROUP)]
        span = jnp.where(
            lane < 2 * ROWS,
            jnp.where(lane < ROWS, span_of[0], span_of[1]),
            jnp.where(lane < 3 * ROWS, span_of[2], span_of[3]),
        )
        into_segment = (offset[0] + block * ROWS + row_in_block) & (SEGMENT - 1)
        lowest = query_row - jnp.minimum(span - 1, into_segment)
        lowest = jnp.maximum(lowest, (OWN - block) * ROWS)
        keys = kv[g, 0]
        values = kv[g, 1]
        queries = qv[heads(g)].reshape(LANES, WIDTH)
        grads = gv[heads(g)].reshape(LANES, WIDTH)
        last = (((1,), (1,)), ((), ()))
        first = (((0,), (0,)), ((), ()))
        scores = lax.dot_general(keys, queries, last, preferred_element_type=jnp.float32)
        prob_grad = lax.dot_general(values, grads, last, preferred_element_type=jnp.float32)
        key_row = lax.broadcasted_iota(jnp.int32, (WINDOW, LANES), 0)
        visible = (key_row >= lowest) & (key_row <= query_row)
        scores = jnp.where(visible, scores, HIDDEN)
        row_max = jnp.max(scores, axis=0, keepdims=True)
        weights = jnp.exp2((scores - row_max) * (scale * LOG2E))
        inverse = 1.0 / jnp.sum(weights, axis=0, keepdims=True)
        row_delta = jnp.sum(weights * prob_grad, axis=0, keepdims=True) * inverse
        probs = (weights * inverse).astype(jnp.bfloat16)
        score_grad = (weights * ((prob_grad - row_delta) * (inverse * scale))).astype(jnp.bfloat16)
        dkey = jnp.dot(score_grad, queries, preferred_element_type=jnp.float32)
        dvalue = jnp.dot(probs, grads, preferred_element_type=jnp.float32)
        for j, s in enumerate((1, 3)):
            rows = slice(s * ROWS, (s + 1) * ROWS)
            xs[g, j, 0] = dkey[rows].astype(jnp.bfloat16)
            xs[g, j, 1] = dvalue[rows].astype(jnp.bfloat16)
        cross(g).start()
        for j, s in enumerate((0, 2, 4)):
            rows = slice(s * ROWS, (s + 1) * ROWS)
            part[g, j, 0] = dkey[rows]
            part[g, j, 1] = dvalue[rows]
        attn = lax.dot_general(
            values, weights.astype(jnp.bfloat16), first, preferred_element_type=jnp.float32
        ) * inverse
        attn_v[heads(g)] = attn.T.astype(jnp.bfloat16).reshape(PER_GROUP, ROWS, WIDTH)
        dquery = lax.dot_general(keys, score_grad, first, preferred_element_type=jnp.float32)
        dq_v[heads(g)] = dquery.T.astype(jnp.bfloat16).reshape(PER_GROUP, ROWS, WIDTH)

    def send_t1(g, total):
        t1[g] = total.astype(jnp.bfloat16)
        chain1(g).start()

    def on_cross(g):
        cross_in(g).wait_recv()
        direct = g >= GROUPS - DIRECT_GRADS

        @pl.when(two_before)
        def _():
            t2[g] = (part[g, 0] + xr[g, 0].astype(jnp.float32)).astype(jnp.bfloat16)
            pl.when(direct)(lambda: chain2_direct(g).start())
            pl.when(jnp.logical_not(direct))(lambda: chain2(g).start())

        @pl.when(has_before & direct)
        def _():
            send_t1(g, part[g, 1] + xr[g, 1].astype(jnp.float32))

    def on_chain2(g):
        @pl.when(has_before & (g < GROUPS - DIRECT_GRADS))
        def _():
            pl.when(has_after)(lambda: chain2(g).wait_recv())
            send_t1(g, part[g, 1] + xr[g, 1].astype(jnp.float32) + ra[g].astype(jnp.float32))

    def on_chain1(g):
        direct = g >= GROUPS - DIRECT_GRADS
        pl.when(has_after)(lambda: chain1(g).wait_recv())
        pl.when(two_after & direct)(lambda: chain2_direct(g).wait_recv())
        total = part[g, 2] + xr[g, 2].astype(jnp.float32) + rb[g].astype(jnp.float32)
        extra = ra[g].astype(jnp.float32)
        total = total + jnp.where(direct, extra, jnp.zeros_like(extra))
        dk_v[g] = total[0].astype(jnp.bfloat16)
        dv_v[g] = total[1].astype(jnp.bfloat16)

    loads[0].wait()
    loads[1].wait()
    pl.semaphore_wait(barrier, 1 + jnp.minimum(here, 2) + jnp.minimum(count - 1 - here, 2))

    for g in range(AHEAD):
        pl.when(has_after)(lambda g=g: hop1(g).start())
        if g < DIRECT_KEYS:
            pl.when(two_after)(lambda g=g: hop2_direct(g).start())

    works = (on_hop1, on_hop2, compute, on_cross, on_chain2, on_chain1)
    stages = tuple(zip(works, LEADS[:2] + (0,) + LEADS[2:]))

    def turn(t, carry):
        for stage, lead in stages:
            g = t + lead

            @pl.when((g >= 0) & (g < GROUPS))
            def _(stage=stage, g=g):
                stage(g)

        return carry

    lax.fori_loop(-LEADS[0], GROUPS - LEADS[-1], turn, 0)

    def finish(g, carry):
        pl.when(has_after)(lambda: hop1(g).wait_send())
        relayed = g >= DIRECT_KEYS
        pl.when((relayed & has_before & has_after) | (jnp.logical_not(relayed) & two_after))(
            lambda: hop2(g).wait_send()
        )
        pair_near(g).wait_send()
        pair_far(g).wait_send()
        cross(g).wait_send()
        pl.when(two_before)(lambda: chain2(g).wait_send())
        pl.when(has_before)(lambda: chain1(g).wait_send())
        return carry

    lax.fori_loop(0, GROUPS, finish, 0)


def flush(*refs):
    copies = []
    for i, pieces in enumerate((4, 4, 1, 1)):
        rows = refs[i].shape[0] // pieces
        for j in range(pieces):
            part = pl.ds(j * rows, rows)
            sem = refs[8].at[i, j]
            copies.append(pltpu.make_async_copy(refs[i].at[part], refs[4 + i].at[part], sem))
    for copy in copies:
        copy.start()
    for copy in copies:
        copy.wait()


def shards(query_matrix, key_matrix, value_matrix, output_gradient, query_head_spans, slab_offset):
    any_space = pl.BlockSpec(memory_space=pl.ANY)
    vmem_space = pl.BlockSpec(memory_space=pltpu.VMEM)
    half = jnp.bfloat16
    group_sems = pltpu.SemaphoreType.DMA((GROUPS,))
    shapes = [
        jax.ShapeDtypeStruct(a.shape, a.dtype)
        for a in (query_matrix, query_matrix, key_matrix, value_matrix)
    ]
    results = pl.pallas_call(
        kernel,
        out_shape=[pltpu.VMEM(a.shape, a.dtype) for a in shapes],
        in_specs=[any_space] * 6,
        out_specs=[vmem_space] * 4,
        scratch_shapes=[
            pltpu.VMEM(query_matrix.shape, half),
            pltpu.VMEM(query_matrix.shape, half),
            pltpu.VMEM((GROUPS, 2, WINDOW, WIDTH), half),
            pltpu.VMEM((GROUPS, 3, 2, ROWS, WIDTH), jnp.float32),
            pltpu.VMEM((GROUPS, 2, 2, ROWS, WIDTH), half),
            pltpu.VMEM((GROUPS, 3, 2, ROWS, WIDTH), half),
            pltpu.VMEM((GROUPS, 2, ROWS, WIDTH), half),
            pltpu.VMEM((GROUPS, 2, ROWS, WIDTH), half),
            pltpu.VMEM((GROUPS, 2, ROWS, WIDTH), half),
            pltpu.VMEM((GROUPS, 2, ROWS, WIDTH), half),
            pltpu.SMEM((GROUPS * PER_GROUP,), jnp.int32),
            pltpu.SMEM((1,), jnp.int32),
            pltpu.SemaphoreType.DMA((6,)),
        ]
        + [group_sems] * 14,
        compiler_params=pltpu.CompilerParams(
            collective_id=0,
            has_side_effects=True,
        ),
    )(query_matrix, key_matrix, value_matrix, output_gradient, query_head_spans, slab_offset)
    return pl.pallas_call(
        flush,
        out_shape=shapes,
        in_specs=[vmem_space] * 4,
        out_specs=[any_space] * 4,
        scratch_shapes=[pltpu.SemaphoreType.DMA((4, 4))],
    )(*[pltpu.with_memory_space_constraint(r, pltpu.VMEM) for r in results])


def solution(mesh):
    blocks = P(None, ("seq", "head"), None)
    return jax.shard_map(
        shards,
        mesh=mesh,
        in_specs=(blocks, blocks, blocks, blocks, P(), P()),
        out_specs=(blocks, blocks, blocks, blocks),
        check_vma=False,
    )
```
